32 devices in a mesh: dp: 4 (over y, x), expert: 8 (over z, core).
Axes of the slice: x: 2, y: 2, z: 4, core: 2. Of those that a mesh axis runs over, the one named last changes fastest.
Arguments:
- tokens: bfloat16 [1536, 2560], P(('dp', 'expert')), may hold values from -6 to 6
- routes: int32 [4, 1536], P(None, ('dp', 'expert')), may hold values from 0 to 1, as said below
- counts: int32 [32, 8], P(('dp', 'expert')), may hold values from 0 to 25, as said below
- router: bfloat16 [2560, 8], P('dp'), may hold values from -0.125 to 0.125
- gate_up_weight: bfloat16 [8, 768, 2, 2560], P('expert', 'dp'), may hold values from -0.125 to 0.125
- down_weight: bfloat16 [8, 768, 2560], P('expert', 'dp'), may hold values from -0.21875 to 0.21875
- cotangent: bfloat16 [4, 1536, 2560], P(None, ('dp', 'expert')), may hold values from -6 to 6
Outputs:
- routed_out: bfloat16 [4, 1536, 2560], P(None, ('dp', 'expert'))
- token_grad: bfloat16 [1536, 2560], P(('dp', 'expert'))
- router_grad: float32 [2560, 8], P('dp', 'expert')
The draws below stay inside these ranges and needn't reach their ends.
Inputs may be any that keep to these rules, and one draw needn't show every extreme that they name: `routes`: within the 48 tokens of one device, no expert of a member is named by more than 25 of that member's copies; in every draw one expert of each member is named by exactly 25 copies on every device. counts[b, m * 2 + l] is the number of tokens of device b (rows b * 48 to (b + 1) * 48 - 1) whose entry of routes for member m is l.
All inputs are finite; a program needn't handle non-finite values.
Results may differ from the reference program's by a relative error of at most 0.0064.
Values may be sent and summed in bfloat16 or wider, within the bound.
No kernel may reach another device: no remote copies, remote signals or barrier semaphores. Data moves between devices by JAX's collectives and lax.ppermute only.
A program may use at most 64 MiB of HBM per device.

```python
import jax
import jax.numpy as jnp
from jax import lax

D = 2560
FFW = 768
MEMBERS = 4
TOK_DEV = 48
EXPERTS = 8
EPM = 2
CAP = 25
TOKENS = 1536
N_DP = 4
N_EXPERT = 8


def route_table(key):
    key = jax.random.fold_in(key, 11)
    key_hot, key_favor, key_noise, key_shuffle = jax.random.split(key, 4)
    blocks = TOKENS // TOK_DEV
    slot_total = EPM * CAP
    slot_expert = jnp.arange(slot_total, dtype=jnp.int32) // CAP
    hot_expert = jax.random.randint(key_hot, (MEMBERS, 1, 1), 0, EPM)
    favor_level = jax.random.randint(key_favor, (MEMBERS, 1, EPM), 0, 4)
    noise_part = jax.random.randint(key_noise, (MEMBERS, blocks, slot_total), 0, 4096)
    scores = jnp.take(favor_level, slot_expert, axis=2) * 1500 + noise_part
    scores = scores + jnp.where(slot_expert[None, None, :] == hot_expert, 65536, 0)
    scores = scores * slot_total + jnp.arange(slot_total, dtype=jnp.int32)[None, None, :]
    _, picked = lax.top_k(scores, TOK_DEV)
    local_ids = picked // CAP
    shuffle_keys = jax.random.randint(key_shuffle, (MEMBERS, blocks, TOK_DEV), 0, 1 << 20) * TOK_DEV + jnp.arange(TOK_DEV, dtype=jnp.int32)[None, None, :]
    shuffle_order = jnp.argsort(shuffle_keys, axis=2)
    local_ids = jnp.take_along_axis(local_ids, shuffle_order, axis=2)
    return local_ids.astype(jnp.int32)


def draw_routes(key, part):
    return route_table(key).reshape(MEMBERS, TOKENS)


def draw_counts(key, part):
    local_ids = route_table(key)
    hit_count = jnp.sum((local_ids[:, :, :, None] == jnp.arange(EPM, dtype=jnp.int32)[None, None, None, :]).astype(jnp.int32), axis=2)
    return jnp.transpose(hit_count, (1, 0, 2)).reshape(TOKENS // TOK_DEV, MEMBERS * EPM)


def levels(rng, dims, cuts, low, high):
    factor_of = 1.0
    for dim, blocks in cuts:
        steps = jax.random.uniform(jax.random.fold_in(jax.random.fold_in(rng, 6), dim), (blocks,), jnp.float32, low / len(cuts), high / len(cuts))
        factor_of = factor_of * jnp.repeat(jnp.exp(steps), dims[dim] // blocks).reshape((-1,) + (1,) * (len(dims) - 1 - dim))
    return factor_of


def gaussian(rng, extent, deviation, reach, pieces=(), held_as=jnp.bfloat16):
    result = deviation * jax.random.normal(rng, extent, jnp.float32)
    if pieces:
        result = result * levels(rng, extent, pieces, -0.22, 0.18)
    return jnp.clip(result, -reach, reach).astype(held_as)


def setup_inputs(seed: int = 0) -> dict:
    seeds = jax.random.split(jax.random.key(seed), 8)
    tokens = gaussian(seeds[0], (TOKENS, D), 1.0, 6.0, ((0, 32),))
    routes = draw_routes(jax.random.fold_in(seeds[7], 71), 0)
    counts = draw_counts(jax.random.fold_in(seeds[7], 71), 0)
    router = gaussian(seeds[3], (D, EXPERTS), D ** -0.5, 0.125, ((0, 4),))
    gate_up_weight = gaussian(seeds[4], (EXPERTS, FFW, 2, D), D ** -0.5, 0.125, ((0, 8), (1, 4)))
    down_weight = gaussian(seeds[5], (EXPERTS, FFW, D), FFW ** -0.5, 0.21875, ((0, 8), (1, 4)))
    cotangent = gaussian(seeds[6], (MEMBERS, TOKENS, D), 1.0, 6.0, ((1, 32),))
    return {"tokens": tokens, "routes": routes, "counts": counts, "router": router, "gate_up_weight": gate_up_weight, "down_weight": down_weight, "cotangent": cotangent}


ROUTE_SCALE = 2.5
BALANCE = 1.0


def expert_pass(tok_rows, grad_rows, gate_weight, up_weight, down_weight):
    contract = (((1,), (1,)), ((), ()))
    gate_pre = lax.dot_general(tok_rows, gate_weight, contract, preferred_element_type=jnp.float32)
    up_pre = lax.dot_general(tok_rows, up_weight, contract, preferred_element_type=jnp.float32)
    squash = jax.nn.sigmoid(gate_pre)
    active = gate_pre * squash
    hidden = (active * up_pre).astype(jnp.bfloat16)
    expert_out = jnp.dot(hidden, down_weight, preferred_element_type=jnp.float32)
    hidden_grad = lax.dot_general(grad_rows, down_weight, contract, preferred_element_type=jnp.float32)
    gate_grad = (hidden_grad * up_pre * squash * (1.0 + gate_pre * (1.0 - squash))).astype(jnp.bfloat16)
    up_grad = (hidden_grad * active).astype(jnp.bfloat16)
    input_grad = jnp.dot(gate_grad, gate_weight, preferred_element_type=jnp.float32) + jnp.dot(up_grad, up_weight, preferred_element_type=jnp.float32)
    return expert_out, input_grad


def reference(tokens, routes, counts, router, gate_up_weight, down_weight, cotangent):
    members, tok_count = routes.shape
    experts = router.shape[1]
    per_member = experts // members
    model_width = tokens.shape[1]
    logits = jnp.dot(tokens, router, preferred_element_type=jnp.float32)
    affinity = jax.nn.sigmoid(logits)
    owners = (routes + per_member * jnp.arange(members, dtype=jnp.int32)[:, None]).astype(jnp.int32)
    gate_values = jnp.take_along_axis(affinity, owners.T, axis=1).T
    out_grad = (ROUTE_SCALE * gate_values[:, :, None] * cotangent.astype(jnp.float32)).astype(jnp.bfloat16)
    copy_count = members * tok_count
    flat_owner = owners.reshape(copy_count)
    copy_tokens = jnp.tile(tokens, (members, 1))
    copy_grads = out_grad.reshape(copy_count, model_width)
    sorted_copies = jnp.argsort(flat_owner, stable=True).astype(jnp.int32)
    expert_sizes = jnp.sum((flat_owner[:, None] == jnp.arange(experts, dtype=jnp.int32)[None, :]).astype(jnp.int32), axis=0)
    starts = (jnp.cumsum(expert_sizes) - expert_sizes).astype(jnp.int32)
    most_rows = N_DP * N_EXPERT * CAP
    lane_index = jnp.arange(most_rows, dtype=jnp.int32)

    def one_expert(buffers, expert_id):
        out_buffer, grad_buffer = buffers
        is_live = lane_index < expert_sizes[expert_id]
        position = jnp.minimum(starts[expert_id] + lane_index, copy_count - 1).astype(jnp.int32)
        picked = sorted_copies[position]
        target = jnp.where(is_live, picked, copy_count).astype(jnp.int32)
        tok_rows = jnp.where(is_live[:, None], copy_tokens[picked], jnp.zeros((), jnp.bfloat16))
        grad_rows = jnp.where(is_live[:, None], copy_grads[picked], jnp.zeros((), jnp.bfloat16))
        pair_weight = gate_up_weight[expert_id]
        expert_out, input_grad = expert_pass(tok_rows, grad_rows, pair_weight[:, 0, :], pair_weight[:, 1, :], down_weight[expert_id])
        out_buffer = out_buffer.at[target].set(expert_out.astype(jnp.bfloat16), mode="drop")
        grad_buffer = grad_buffer.at[target].set(input_grad.astype(jnp.bfloat16), mode="drop")
        return (out_buffer, grad_buffer), None

    blank = jnp.zeros((copy_count, model_width), jnp.bfloat16)
    (copy_out, copy_back), _ = lax.scan(one_expert, (blank, blank), jnp.arange(experts, dtype=jnp.int32))
    expert_out = copy_out.reshape(members, tok_count, model_width)
    routed_out = (ROUTE_SCALE * gate_values[:, :, None] * expert_out.astype(jnp.float32)).astype(jnp.bfloat16)
    affinity_grad = ROUTE_SCALE * jnp.sum(cotangent.astype(jnp.float32) * expert_out.astype(jnp.float32), axis=2)
    expert_load = jnp.sum(counts, axis=0)
    balance = per_member * expert_load.astype(jnp.float32) / tok_count
    chosen = (owners[:, :, None] == jnp.arange(experts, dtype=jnp.int32)[None, None, :]).astype(jnp.float32)
    routed_grad = jnp.sum(chosen * affinity_grad[:, :, None], axis=0)
    logit_grad = (affinity * (1.0 - affinity) * (BALANCE * balance[None, :] + routed_grad)).astype(jnp.bfloat16)
    back_sum = jnp.sum(copy_back.reshape(members, tok_count, model_width).astype(jnp.float32), axis=0)
    router_back = lax.dot_general(logit_grad, router, (((1,), (1,)), ((), ())), preferred_element_type=jnp.float32)
    token_grad = (back_sum + router_back).astype(jnp.bfloat16)
    router_grad = lax.dot_general(tokens, logit_grad, (((0,), (0,)), ((), ())), preferred_element_type=jnp.float32) * (tok_count ** -0.5)
    return routed_out, token_grad, router_grad
```

```python
import jax
import jax.numpy as jnp
from jax import lax
from jax.sharding import PartitionSpec as P

ROUTE_SCALE = 2.5
BALANCE = 1.0
ROWS_BY_ROWS = (((1,), (1,)), ((), ()))
FIRST_AXIS = (((0,), (0,)), ((), ()))


def expert_pass(tok_rows, grad_rows, gate_weight, up_weight, down_weight):
    contract = (((1,), (1,)), ((), ()))
    gate_pre = lax.dot_general(tok_rows, gate_weight, contract, preferred_element_type=jnp.float32)
    up_pre = lax.dot_general(tok_rows, up_weight, contract, preferred_element_type=jnp.float32)
    squash = jax.nn.sigmoid(gate_pre)
    active = gate_pre * squash
    hidden = (active * up_pre).astype(jnp.bfloat16)
    expert_out = jnp.dot(hidden, down_weight, preferred_element_type=jnp.float32)
    hidden_grad = lax.dot_general(
        grad_rows, down_weight, contract, preferred_element_type=jnp.float32
    )
    gate_grad = (hidden_grad * up_pre * squash * (1.0 + gate_pre * (1.0 - squash))).astype(
        jnp.bfloat16
    )
    up_grad = (hidden_grad * active).astype(jnp.bfloat16)
    input_grad = jnp.dot(gate_grad, gate_weight, preferred_element_type=jnp.float32) + jnp.dot(
        up_grad, up_weight, preferred_element_type=jnp.float32
    )
    return (expert_out, input_grad)


def routed_plan(tokens, routes, counts, router, gate_up_weight, down_weight, cotangent):
    members, tok_local = routes.shape
    model_width = tokens.shape[1]
    experts = router.shape[1]
    per_member = experts // members
    capacity = max(2, tok_local // per_member + 1)
    slot_total = experts * capacity
    copy_count = members * tok_local
    tok_total = tok_local * lax.axis_size("dp") * lax.axis_size("expert")
    router_full = lax.all_gather(router, "dp", axis=0, tiled=True)
    logits = jnp.dot(tokens, router_full, preferred_element_type=jnp.float32)
    affinity = jax.nn.sigmoid(logits)
    owners = routes + per_member * jnp.arange(members, dtype=jnp.int32)[:, None]
    expert_ids = jnp.arange(experts, dtype=jnp.int32)
    chosen = (owners[:, :, None] == expert_ids[None, None, :]).astype(jnp.float32)
    gate_values = jnp.sum(chosen * affinity[None, :, :], axis=2)
    out_grad = (ROUTE_SCALE * gate_values[:, :, None] * cotangent.astype(jnp.float32)).astype(
        jnp.bfloat16
    )
    flat_owner = owners.reshape(copy_count)
    owner_hits = (flat_owner[:, None] == expert_ids[None, :]).astype(jnp.int32)
    rank_index = jnp.cumsum(owner_hits, axis=0) - 1
    slot_of = jnp.sum(owner_hits * rank_index, axis=1)
    target = flat_owner * capacity + slot_of
    placing = (jnp.arange(slot_total, dtype=jnp.int32)[:, None] == target[None, :]).astype(
        jnp.bfloat16
    )
    per_token = jnp.sum(placing.reshape(slot_total, members, tok_local), axis=1)
    send_tokens = (
        jnp.dot(per_token, tokens, preferred_element_type=jnp.float32)
        .astype(jnp.bfloat16)
        .reshape(experts, capacity, model_width)
    )
    send_grads = (
        jnp.dot(
            placing, out_grad.reshape(copy_count, model_width), preferred_element_type=jnp.float32
        )
        .astype(jnp.bfloat16)
        .reshape(experts, capacity, model_width)
    )
    recv_tokens, recv_grads = (
        lax.all_to_all(send_tokens, "expert", split_axis=0, concat_axis=0, tiled=True),
        lax.all_to_all(send_grads, "expert", split_axis=0, concat_axis=0, tiled=True),
    )
    tok_rows = recv_tokens.reshape(slot_total, model_width)
    grad_rows = recv_grads.reshape(slot_total, model_width)
    pair_piece = lax.all_gather(gate_up_weight, "dp", axis=1, tiled=True)
    down_piece = lax.all_gather(down_weight, "dp", axis=1, tiled=True)
    expert_out, input_grad = expert_pass(
        tok_rows, grad_rows, pair_piece[0, :, 0, :], pair_piece[0, :, 1, :], down_piece[0]
    )
    ret_out = expert_out.astype(jnp.bfloat16).reshape(experts, capacity, model_width)
    ret_grad = input_grad.astype(jnp.bfloat16).reshape(experts, capacity, model_width)
    back_out, back_grad = (
        lax.all_to_all(ret_out, "expert", split_axis=0, concat_axis=0, tiled=True),
        lax.all_to_all(ret_grad, "expert", split_axis=0, concat_axis=0, tiled=True),
    )
    first_axis = (((0,), (0,)), ((), ()))
    copy_out = (
        lax.dot_general(
            placing,
            back_out.reshape(slot_total, model_width),
            first_axis,
            preferred_element_type=jnp.float32,
        )
        .astype(jnp.bfloat16)
        .reshape(members, tok_local, model_width)
    )
    back_sum = lax.dot_general(
        per_token,
        back_grad.reshape(slot_total, model_width),
        first_axis,
        preferred_element_type=jnp.float32,
    )
    routed_out = (ROUTE_SCALE * gate_values[:, :, None] * copy_out.astype(jnp.float32)).astype(
        jnp.bfloat16
    )
    affinity_grad = ROUTE_SCALE * jnp.sum(
        cotangent.astype(jnp.float32) * copy_out.astype(jnp.float32), axis=2
    )
    expert_load = lax.psum(counts[0], ("dp", "expert"))
    balance = per_member * expert_load.astype(jnp.float32) / tok_total
    routed_grad = jnp.sum(chosen * affinity_grad[:, :, None], axis=0)
    logit_grad = (affinity * (1.0 - affinity) * (BALANCE * balance[None, :] + routed_grad)).astype(
        jnp.bfloat16
    )
    router_back = lax.dot_general(
        logit_grad, router_full, (((1,), (1,)), ((), ())), preferred_element_type=jnp.float32
    )
    token_grad = (back_sum + router_back).astype(jnp.bfloat16)
    partial_grad = lax.dot_general(
        tokens, logit_grad, first_axis, preferred_element_type=jnp.float32
    ) * tok_total ** (-0.5)
    column_share = lax.psum_scatter(partial_grad, "expert", scatter_dimension=1, tiled=True)
    router_grad = lax.psum_scatter(column_share, "dp", scatter_dimension=0, tiled=True)
    return (routed_out, token_grad, router_grad)


def column_plan(tokens, routes, counts, router, gate_up_weight, down_weight, cotangent):
    members, tok_local = routes.shape
    width = tokens.shape[1]
    experts = router.shape[1]
    per_member = experts // members
    n_dp, n_expert = lax.axis_size("dp"), lax.axis_size("expert")
    rows = n_expert * (tok_local // per_member + 1)
    column = n_expert * tok_local
    half = column // 2
    tok_total = tok_local * n_dp * n_expert
    d, e = lax.axis_index("dp"), lax.axis_index("expert")
    member, core = e // per_member, e % per_member
    f32, bf16 = jnp.float32, jnp.bfloat16

    def over_expert(v, k):
        return lax.ppermute(v, "expert", [(i, i ^ k) for i in range(n_expert)])

    def over_dp(v, k):
        return lax.ppermute(v, "dp", [(i, i ^ k) for i in range(n_dp)])

    def crossed(v, by_core):
        pairs = []
        for i in range(n_dp):
            for j in range(n_expert):
                pairs.append((i * n_expert + j, (i ^ by_core[j % per_member]) * n_expert + j))
        return lax.ppermute(v, ("dp", "expert"), pairs)

    def over_weights(v):
        return crossed(v, (1, 2))

    def over_rows(v):
        return crossed(v, (2, 1))

    def column_gather(v, axis=0):
        for k in (4, 2, 1):
            v = jnp.concatenate([v, over_expert(v, k)], axis=axis)
        return v

    gate_up_far = over_weights(gate_up_weight)
    down_far = over_weights(down_weight)
    col_tokens = column_gather(tokens)

    def of_member(v, k):
        return lax.dynamic_index_in_dim(v, member ^ (k // per_member), 0, keepdims=False)

    grads = [of_member(cotangent, 0)]
    for k in (4, 2, 6):
        grads.append(over_expert(of_member(cotangent, k), k))
    col_grads = jnp.concatenate(grads, axis=0)
    col_grads = jnp.concatenate([col_grads, over_expert(col_grads, 1)], axis=0)

    small = jnp.concatenate([routes.reshape(1, members * tok_local), counts], axis=1)
    small = column_gather(small)
    load = jnp.sum(small[:, members * tok_local :], axis=0, keepdims=True)
    for k in (1, 2):
        load = load + over_dp(load, k)
    col_routes = small[:, : members * tok_local].reshape(n_expert, members, tok_local)
    col_routes = lax.dynamic_index_in_dim(col_routes, member, 1, keepdims=False).reshape(column)

    router_t = router.T
    for k in (1, 2):
        other = over_dp(router_t, k)
        high = (d & k) != 0
        router_t = jnp.concatenate(
            [jnp.where(high, other, router_t), jnp.where(high, router_t, other)], axis=1
        )
    mine = (jnp.arange(experts, dtype=jnp.int32) == e).astype(f32)

    hit = col_routes == core
    slot = jnp.cumsum(hit.astype(jnp.int32)) - 1
    placed = (jnp.arange(rows, dtype=jnp.int32)[:, None] == slot[None, :]) & hit[None, :]
    placing = placed.astype(bf16)
    logits = lax.dot_general(col_tokens, router_t, ROWS_BY_ROWS, preferred_element_type=f32)
    affinity = jnp.sum(jax.nn.sigmoid(logits) * mine[None, :], axis=1)
    gate_rows = jnp.sum(jnp.where(placed, affinity[None, :], 0.0), axis=1, keepdims=True)
    tok_rows = jnp.dot(placing, col_tokens, preferred_element_type=f32).astype(bf16)
    tok_rows_far = over_rows(tok_rows)
    cot_rows = jnp.dot(placing, col_grads, preferred_element_type=f32).astype(bf16)
    grad_rows = (ROUTE_SCALE * gate_rows * cot_rows.astype(f32)).astype(bf16)
    grad_rows_far = over_rows(grad_rows)

    gates = (gate_up_weight[0, :, 0, :], gate_up_far[0, :, 0, :])
    ups = (gate_up_weight[0, :, 1, :], gate_up_far[0, :, 1, :])
    downs = (down_weight[0], down_far[0])

    def forward(x):
        total, kept = None, []
        for gate, up, down in zip(gates, ups, downs):
            g = lax.dot_general(x, gate, ROWS_BY_ROWS, preferred_element_type=f32)
            u = lax.dot_general(x, up, ROWS_BY_ROWS, preferred_element_type=f32)
            hidden = (g * jax.nn.sigmoid(g) * u).astype(bf16)
            part = jnp.dot(hidden, down, preferred_element_type=f32)
            total = part if total is None else total + part
            kept.append((g, u))
        return total, kept

    def backward(y, kept):
        total = None
        for gate, up, down, (g, u) in zip(gates, ups, downs, kept):
            s = jax.nn.sigmoid(g)
            hg = lax.dot_general(y, down, ROWS_BY_ROWS, preferred_element_type=f32)
            gate_grad = (hg * u * s * (1.0 + g * (1.0 - s))).astype(bf16)
            up_grad = (hg * g * s).astype(bf16)
            part = jnp.dot(gate_grad, gate, preferred_element_type=f32) + jnp.dot(
                up_grad, up, preferred_element_type=f32
            )
            total = part if total is None else total + part
        return total

    out_far, kept_far = forward(tok_rows_far)
    out_back = over_rows(out_far.astype(bf16))
    out_near, kept_near = forward(tok_rows)
    grad_far = backward(grad_rows_far, kept_far)
    grad_back = over_rows(grad_far.astype(bf16))
    grad_near = backward(grad_rows, kept_near)

    out_rows = (out_near + out_back.astype(f32)).astype(bf16)
    routed_rows = (ROUTE_SCALE * gate_rows * out_rows.astype(f32)).astype(bf16)
    routed_col = lax.dot_general(
        placing, routed_rows, FIRST_AXIS, preferred_element_type=f32
    ).astype(bf16)
    routed = routed_col[:half] + over_expert(routed_col[half:], 1)
    routed = routed.reshape(members, tok_local, width)
    parts = [routed[0], over_expert(routed[2], 2), over_expert(routed[1], 4), over_expert(routed[3], 6)]
    for bit in (1, 2):
        odd = (member & bit) != 0
        parts = [jnp.where(odd, parts[i ^ bit], parts[i]) for i in range(members)]
    routed_out = jnp.stack(parts)

    affinity_grad = ROUTE_SCALE * jnp.sum(
        cot_rows.astype(f32) * out_rows.astype(f32), axis=1, keepdims=True
    )
    routed_grad = jnp.sum(jnp.where(placed, affinity_grad, 0.0), axis=0)
    balance = per_member * load.astype(f32) / tok_total
    balance = jnp.sum(balance[0] * mine)
    logit_grad = (affinity * (1.0 - affinity) * (BALANCE * balance + routed_grad)).astype(bf16)
    column_grad = lax.dot_general(
        logit_grad[None, :], col_tokens, (((1,), (0,)), ((), ())), preferred_element_type=f32
    ) * tok_total ** (-0.5)
    for k in (1, 2):
        column_grad = column_grad + over_dp(column_grad, k)
    share = width // n_dp
    router_grad = lax.dynamic_slice_in_dim(column_grad, d * share, share, axis=1).reshape(share, 1)

    router_row = jnp.sum(router_t.astype(f32) * mine[:, None], axis=0, keepdims=True)
    grad_rows_out = (grad_near + grad_back.astype(f32)).astype(bf16)
    grad_col = lax.dot_general(placing, grad_rows_out, FIRST_AXIS, preferred_element_type=f32)
    grad_col = grad_col + logit_grad.astype(f32)[:, None] * router_row
    swapped = over_expert(grad_col[half:].astype(bf16), 1)
    back = (grad_col[:half] + swapped.astype(f32)).astype(bf16)
    quarter = half // 2
    back = (
        back[:quarter].astype(f32) + over_expert(back[quarter:], 2).astype(f32)
    )
    moved = over_expert(back[tok_local:].astype(bf16), 4)
    token_grad = (back[:tok_local] + moved.astype(f32)).astype(bf16)
    return routed_out, token_grad, router_grad


def solution(mesh):
    n_dp, n_expert = mesh.shape["dp"], mesh.shape["expert"]

    def on_device(tokens, routes, counts, router, gate_up_weight, down_weight, cotangent):
        members, experts = routes.shape[0], router.shape[1]
        fits = members == 4 and experts == 8 and n_expert == experts and n_dp == 4
        plan = column_plan if fits else routed_plan
        return plan(tokens, routes, counts, router, gate_up_weight, down_weight, cotangent)

    in_specs = (
        P(("dp", "expert"), None),
        P(None, ("dp", "expert")),
        P(("dp", "expert"), None),
        P("dp", None),
        P("expert", "dp", None, None),
        P("expert", "dp", None),
        P(None, ("dp", "expert"), None),
    )
    out_specs = (P(None, ("dp", "expert"), None), P(("dp", "expert"), None), P("dp", "expert"))
    return jax.shard_map(
        on_device, mesh=mesh, in_specs=in_specs, out_specs=out_specs, check_vma=False
    )
```
